128 devices in a mesh: sect: 4 (over x), dom: 32 (over z, y, core).
Axes of the slice: x: 4, y: 4, z: 4, core: 2. Of those that a mesh axis runs over, the one named last changes fastest.
Arguments:
- fluid_source: float32 [16384, 32, 128], P(('sect', 'dom')), may hold values from -8 to 8
- coef_ids: int32 [16384, 32, 128], P(('sect', 'dom')), may hold values from 0 to 15
- coef_table: float32 [16], replicated, may hold values from 0.5 to 8
- owner_device: int32 [16384, 1], P(('sect', 'dom')), may hold values from 0 to 127; in each aligned block of 128 rows (0 to 127, 128 to 255, ...) at most 2 rows name the same one
- owner_slot: int32 [16384, 1], P(('sect', 'dom')), may hold values from 0 to 127
- solid_init: float32 [16384, 128], P(('sect', 'dom')), may hold values from -4 to 4
- solid_load: float32 [16384, 128], P(('sect', 'dom')), may hold values from -6 to 6
- compliance: float32 [128, 128], replicated, may hold values from -0.5 to 0.5
Outputs:
- fluid_state: float32 [16384, 32, 128], P(('sect', 'dom'))
- displacement: float32 [16384, 128], P(('sect', 'dom'))
- coupling_norms: float32 [2], replicated
The draws below stay inside these ranges and needn't reach their ends.
Inputs may be any that keep to these rules, and one draw needn't show every extreme that they name: `owner_device`: among the 128 rows of one device no owner device is named more than 2 times, a bound that some block reaches.
All inputs are finite; a program needn't handle non-finite values.
Results may differ from the reference program's by a relative error of at most 0.0001.
Values sent between devices are 32-bit elements; how exact they have to be, the bound alone decides.
No kernel may reach another device: no remote copies, remote signals or barrier semaphores. Data moves between devices by JAX's collectives and lax.ppermute only.
A program may use at most 64 MiB of HBM per device.

```python
import math
import jax
import jax.numpy as jnp
import numpy as np
from jax import lax

ROW = 128
FX = 128
FY = 32
SDEV = 128
NCOEF = 16
SWEEPS = 3
COUPLE = 2
CAP = 2
NXF = 16384
NS = 16384
DEVICES = 128


def set_ends(array, rng, smallest, high):
    index_at = [jax.random.randint(jax.random.fold_in(rng, axis), (), 0, length) for axis, length in enumerate(array.shape)]
    main_axis = array.shape.index(max(array.shape))
    beside = index_at[:main_axis] + [(index_at[main_axis] + 1) % array.shape[main_axis]] + index_at[main_axis + 1:]
    return array.at[tuple(index_at)].set(smallest).at[tuple(beside)].set(high)


def shard_levels(rng, dims, shards, low, high):
    def one(position, parts):
        draws = jax.random.uniform(jax.random.fold_in(jax.random.fold_in(rng, 6), position), (parts,), jnp.float32, low / len(shards), high / len(shards))
        return jnp.repeat(jnp.exp(draws), dims[position] // parts).reshape((-1,) + (1,) * (len(dims) - position - 1))

    loudness = one(*shards[0])
    for cut in shards[1:]:
        loudness = loudness * one(*cut)
    return loudness


def routed_block(key, own, number, rows, amount, top, reach, skew):
    order = jax.random.permutation(key, amount)
    crowded, ordinary = portions_of(amount, rows * top, reach, skew, True), portions_of(amount, rows * top, reach, skew, False)
    places = jnp.arange(amount)

    def named(tallies, turn):
        used = int((tallies > 0).sum())
        fixed = max(1, used // 4)
        moved = fixed + (places - fixed + turn * (used - fixed)) % max(1, amount - fixed)
        return jnp.zeros((amount,), jnp.int32).at[order[jnp.where(places < fixed, places, moved)]].set(jnp.asarray(tallies, jnp.int32))

    tallies = jnp.where(number % 4 == 0, named(crowded, number // 4), named(ordinary, number - number // 4 - 1))
    mixed = jax.random.permutation(jax.random.fold_in(own, 3), amount)
    giver, sink = mixed[0:amount // 2 * 2:2], mixed[1:amount // 2 * 2:2]
    slack = jnp.minimum(tallies[giver] - 1, reach - tallies[sink]) // 2
    slack = jnp.where((giver == order[0]) | (sink == order[0]) | (tallies[sink] == 0), 0, jnp.maximum(slack, 0))
    moved = jax.random.randint(jax.random.fold_in(own, 4), (amount // 2,), 0, 1 << 20) % (slack + 1)
    tallies = tallies.at[giver].add(-moved).at[sink].add(moved)
    labels = jnp.searchsorted(jnp.cumsum(tallies), jnp.arange(rows * top), side="right").astype(jnp.int32)
    grid = labels.reshape(top, rows).T
    grid = grid[jax.random.permutation(jax.random.fold_in(own, 1), rows)]
    turn = jax.random.randint(jax.random.fold_in(own, 2), (rows, 1), 0, top)
    return jnp.take_along_axis(grid, (jnp.arange(top)[None, :] + turn) % top, axis=1)


def portions_of(count, total, reach, skew, full):
    loads = [(1 << 20) // math.isqrt(grade ** skew) + 1 for grade in range(1, count + 1)]
    largest = reach if full else min(reach, max(-(-total // count), total * loads[0] // sum(loads)))
    least = 1 if total - largest >= count - 1 else 0
    given, rest = [largest] + [least] * (count - 1), total - largest - least * (count - 1)
    while rest > 0:
        free = [i for i in range(1, count) if given[i] < largest] or [i for i in range(1, count) if given[i] < reach]
        mass, remaining = sum([loads[i] for i in free]), rest
        for i in free:
            more = min(reach - given[i], max(1, remaining * loads[i] // mass), rest)
            given[i] = given[i] + more
            rest = rest - more
    return np.array(given)


def normal_values(key, extent, width, bound, split=(), held_as=jnp.bfloat16):
    factor_of = shard_levels(key, extent, split, -0.22, 0.18) if split else 1.0
    entries = jax.random.normal(key, extent, jnp.float32) * width * factor_of
    return jnp.minimum(jnp.maximum(entries, -bound), bound).astype(held_as)


def setup_inputs(seed: int = 0) -> dict:
    arg_keys = jax.random.split(jax.random.key(seed), 9)
    fluid_source = normal_values(arg_keys[0], (NXF, FY, ROW), 1.0, 8.0, ((0, 128),), jnp.float32)
    coef_ids = set_ends(jax.random.randint(arg_keys[1], (NXF, FY, ROW), 0, NCOEF), jax.random.fold_in(arg_keys[1], 1), 0, NCOEF - 1).astype(jnp.int32)
    coef_table = jnp.clip(jnp.exp(jax.random.uniform(arg_keys[2], (NCOEF,), jnp.float32, math.log(0.5), math.log(8.0))), 0.5, 8.0)
    owner_device_keys = jax.random.split(jax.random.fold_in(arg_keys[3], 1), NXF // FX)
    owner_device_turns = jax.random.permutation(jax.random.fold_in(arg_keys[3], 3), NXF // FX)
    owner_device = jax.vmap(lambda own, number: routed_block(jax.random.fold_in(arg_keys[3], 2), own, number, FX, DEVICES, 1, CAP, 2))(owner_device_keys, owner_device_turns).reshape((NXF, 1))
    owner_slot = set_ends(jax.random.randint(arg_keys[4], (NXF, 1), 0, SDEV), jax.random.fold_in(arg_keys[4], 1), 0, SDEV - 1).astype(jnp.int32)
    solid_init = normal_values(arg_keys[5], (NS, ROW), 0.5, 4.0, ((0, 128),), jnp.float32)
    solid_load = normal_values(arg_keys[6], (NS, ROW), 1.0, 6.0, ((0, 128),), jnp.float32)
    compliance = normal_values(arg_keys[7], (ROW, ROW), ROW ** -0.5, 0.5, (), jnp.float32)
    return dict(fluid_source=fluid_source, coef_ids=coef_ids, coef_table=coef_table, owner_device=owner_device, owner_slot=owner_slot, solid_init=solid_init, solid_load=solid_load, compliance=compliance)


def neighbours(fluid_state):
    padded = jnp.pad(fluid_state, 1)
    total = padded[2:, 1:-1, 1:-1] + padded[:-2, 1:-1, 1:-1]
    total = total + padded[1:-1, 2:, 1:-1] + padded[1:-1, :-2, 1:-1]
    total = total + padded[1:-1, 1:-1, 2:] + padded[1:-1, 1:-1, :-2]
    return total

def reference(fluid_source, coef_ids, coef_table, owner_device, owner_slot, solid_init, solid_load, compliance):
    diagonal = 6.0 + coef_table[coef_ids]
    target_row = (owner_device[:, 0] * SDEV + owner_slot[:, 0]).astype(jnp.int32)
    fluid_state = jnp.zeros(fluid_source.shape, jnp.float32)
    displacement = solid_init
    norm_list = []
    for iteration in range(COUPLE):
        wall_rows = displacement[target_row]
        source = fluid_source.at[:, 0, :].add(wall_rows)
        for sweep_index in range(SWEEPS):
            fluid_state = (source + neighbours(fluid_state)) / diagonal
        traction = fluid_state[:, 0, :] - fluid_state[:, 1, :]
        solid_force = jax.ops.segment_sum(traction, target_row, num_segments=NS) + solid_load
        trial_disp = jnp.dot(solid_force, compliance, precision=lax.Precision.HIGHEST)
        mismatch = trial_disp - displacement
        norm_list.append(jnp.sqrt(jnp.sum(mismatch * mismatch) + 1e-06))
        displacement = displacement + 0.5 * mismatch
    return (fluid_state, displacement, jnp.stack(norm_list))
```

```python
import functools

import jax
import jax.numpy as jnp
from jax import lax
from jax.experimental import pallas as pl
from jax.experimental.pallas import tpu as pltpu
from jax.sharding import PartitionSpec as P

AXES = ("sect", "dom")
SWEEPS = 3
COUPLE = 2
RELAX = 0.5
ROWS = 128
FY = 32
ROW = 128
CAP = 2
SLOTS = 6
REACH = 2
PAD = 8
EXT = ROWS + 2 * PAD
HIGHEST = lax.Precision.HIGHEST
F32 = jnp.float32
CHUNKS = 8
NEAR_LIMIT = 24 * 1024 * 1024
FAR_LIMIT = 65_500_000


def shape(*dims):
    return jax.ShapeDtypeStruct(dims, F32)


def iota(dims, axis):
    return lax.broadcasted_iota(jnp.int32, dims, axis)


def kernel_call(
    body, outs, *args, scratch=(), far=(), far_out=(), alias=None, flops=1e6, moved=1e6, name=None
):
    def spec(is_far):
        return pl.BlockSpec(memory_space=pltpu.HBM if is_far else pltpu.VMEM)

    single = not isinstance(outs, tuple)
    out_specs = [spec(k in far_out) for k in range(1 if single else len(outs))]
    return pl.pallas_call(
        body,
        out_shape=outs,
        in_specs=[spec(k in far) for k in range(len(args))],
        out_specs=out_specs[0] if single else out_specs,
        scratch_shapes=list(scratch),
        input_output_aliases=alias or {},
        compiler_params=pltpu.CompilerParams(vmem_limit_bytes=FAR_LIMIT if far else NEAR_LIMIT),
        cost_estimate=pl.CostEstimate(
            flops=int(flops), bytes_accessed=int(moved), transcendentals=0
        ),
        name=name,
    )(*args)


def dot(a, b):
    return jnp.dot(a, b, precision=HIGHEST, preferred_element_type=F32)


def request_body(od_ref, os_ref, req_ref, poscol_ref, posrow_ref):
    sq = (ROWS, ROWS)
    sub, lane = iota(sq, 0).astype(F32), iota(sq, 1).astype(F32)
    od_r, os_r = od_ref[...].astype(F32), os_ref[...].astype(F32)
    od_c = jnp.sum(jnp.where(sub == lane, od_r, 0.0), axis=1, keepdims=True)
    od_c = jnp.broadcast_to(od_c, sq)
    same = od_c == od_r
    rank_c = jnp.sum(jnp.where(same & (lane < sub), 1.0, 0.0), axis=1, keepdims=True)
    rank_r = jnp.sum(jnp.where(same & (sub < lane), 1.0, 0.0), axis=0, keepdims=True)
    edge = jnp.full((PAD, ROW), -1.0, F32)
    poscol_ref[0:PAD] = edge
    poscol_ref[PAD : PAD + ROWS] = od_c * SLOTS + rank_c
    poscol_ref[PAD + ROWS : EXT] = edge
    posrow_ref[...] = jnp.broadcast_to(od_r * CAP + rank_r, (8, ROWS))
    code_r = os_r * ROWS + lane[0:1] + 1.0
    wanted = od_r == sub
    first = jnp.sum(jnp.where(wanted & (rank_r == 0.0), code_r, 0.0), axis=1, keepdims=True)
    second = jnp.sum(jnp.where(wanted & (rank_r == 1.0), code_r, 0.0), axis=1, keepdims=True)
    req_ref[...] = jnp.where(lane == 0.0, first, jnp.where(lane == 1.0, second, 0.0))


def pick_body(devices, recv_ref, disp_ref, ans_ref, sel_ref, slotrow_ref):
    got = recv_ref[...]
    one = got[:, 0:1] - 1.0
    two = got[:, 1:2] - 1.0
    slot_a, slot_b = jnp.floor(one / ROWS), jnp.floor(two / ROWS)
    row_a, row_b = one - slot_a * ROWS, two - slot_b * ROWS
    slot_a, slot_b = slot_a + 1.0, slot_b + 1.0
    lane = iota((devices, ROW), 1)
    beside = jnp.where(
        lane < 4,
        jnp.where(lane == 2, ROWS - 2.0, ROWS - 1.0),
        jnp.where(lane == 4, 0.0, jnp.where(lane == 5, 1.0, -5.0)),
    )
    halo = jnp.where(row_a == beside, slot_a, 0.0) + jnp.where(row_b == beside, slot_b, 0.0)
    table = jnp.where(lane == 0, slot_a, jnp.where(lane == 1, slot_b, halo))
    count = devices * SLOTS
    index = iota((count, devices), 0)
    target = lax.shift_right_logical(index * 10923, 16)
    kind = index - SLOTS * target
    source = target + jnp.where(kind < 2, 0, jnp.where(kind < 4, -1, 1))
    spread = jnp.where(source == iota((count, devices), 1), 1.0, 0.0)
    spread = jnp.dot(
        spread.astype(jnp.bfloat16), table.astype(jnp.bfloat16), preferred_element_type=F32
    )
    index = iota((count, ROW), 0)
    lanes = iota((count, ROW), 1)
    kind = index - SLOTS * lax.shift_right_logical(index * 10923, 16)
    sel = jnp.sum(jnp.where(lanes == kind, spread, 0.0), axis=1, keepdims=True)
    sel_ref[...] = jnp.broadcast_to(sel, (count, ROW))
    ans_ref[...] = dot(jnp.where(sel == lanes.astype(F32) + 1.0, 1.0, 0.0), disp_ref[...])
    wide = (devices, CAP * devices)
    col = iota(wide, 1)
    value = jnp.where((col & 1) == 0, slot_a, slot_b)
    mine = iota(wide, 0) == lax.shift_right_logical(col, 1)
    slotrow = jnp.sum(jnp.where(mine, value, 0.0), axis=0, keepdims=True)
    slotrow_ref[...] = jnp.broadcast_to(slotrow, (8, CAP * devices))


def solid_core(inc_ref, slotrow_ref, disp_ref, load_ref, comp_ref):
    count = inc_ref.shape[0]
    place = jnp.where(
        slotrow_ref[0:1] == iota((ROWS, count), 0).astype(F32) + 1.0, 1.0, 0.0
    )
    force = dot(place, inc_ref[...]) + load_ref[...]
    disp = disp_ref[...]
    mismatch = dot(force, comp_ref[...]) - disp
    square = mismatch * mismatch
    total = jnp.sum(jnp.sum(square, axis=0, keepdims=True), axis=1, keepdims=True)
    return disp, mismatch, total


def solid_body(
    inc_ref, slotrow_ref, disp_ref, load_ref, comp_ref, sel_ref, after_ref, ans_ref, new_ref,
    part_ref,
):
    disp, mismatch, total = solid_core(inc_ref, slotrow_ref, disp_ref, load_ref, comp_ref)
    new = disp + RELAX * mismatch
    new_ref[...] = new
    part_ref[...] = jnp.broadcast_to(total, part_ref.shape)
    sel = sel_ref[...]
    hot = jnp.where(sel == iota(sel.shape, 1).astype(F32) + 1.0, 1.0, 0.0)
    ans_ref[...] = dot(hot, new)


def last_body(
    devices, inc_ref, slotrow_ref, disp_ref, load_ref, comp_ref, part_ref, after_ref, new_ref,
    norm_ref,
):
    disp, mismatch, total = solid_core(inc_ref, slotrow_ref, disp_ref, load_ref, comp_ref)
    new_ref[...] = disp + RELAX * mismatch
    lane = iota((devices, ROW), 1)
    norm_ref[...] = jnp.where(lane == 0, part_ref[0:1], jnp.where(lane == 1, total, 0.0))


def edges_body(fs_ref, ids_ref, up_ref, down_ref, buf_ref, sem):
    edge = REACH * FY
    copies = []
    for k, at in enumerate((ROWS * FY - edge, 0)):
        out = (up_ref, down_ref)[k]
        copies.append(
            pltpu.make_async_copy(fs_ref.at[pl.ds(at, edge)], out.at[pl.ds(0, edge)], sem.at[2 * k])
        )
        copies.append(
            pltpu.make_async_copy(ids_ref.at[pl.ds(at, edge)], buf_ref.at[k], sem.at[2 * k + 1])
        )
    for copy in copies:
        copy.start()
    for copy in copies:
        copy.wait()
    up_ref[edge:] = buf_ref[0].astype(F32) + 1.0
    down_ref[edge:] = buf_ref[1].astype(F32) + 1.0


def prepare_body(
    fs_hbm, ids_hbm, tab_ref, left_ref, right_ref, after_ref, b_hbm, inv_hbm, bt_ref, it_ref,
    fs_ref, ids_ref, b_ref, inv_ref, sem, osem,
):
    step = ROWS // CHUNKS
    loads = []
    for c in range(CHUNKS):
        part = pl.ds(c * step * FY, step * FY)
        pair = (
            pltpu.make_async_copy(fs_hbm.at[part], fs_ref.at[part], sem.at[0, c]),
            pltpu.make_async_copy(ids_hbm.at[part], ids_ref.at[part], sem.at[1, c]),
        )
        for copy in pair:
            copy.start()
        loads.append(pair)
    tab = jnp.broadcast_to(tab_ref[0:1], (FY, ROW))

    def look(ids):
        return jnp.take_along_axis(tab, ids, axis=1, mode="promise_in_bounds")

    for ref, base in ((left_ref, 0), (right_ref, REACH + ROWS)):
        for k in range(REACH):
            marked = ref[(REACH + k) * FY : (REACH + k + 1) * FY, :].astype(jnp.int32)
            inv = look(jnp.maximum(marked - 1, 0))
            inv = jnp.where(marked > 0, inv, 0.0)
            at = (base + k) * FY
            inv_ref[at : at + FY, :] = inv
            b_ref[at : at + FY, :] = inv * ref[k * FY : (k + 1) * FY, :]

    def plane(x, carry):
        here = pl.ds(pl.multiple_of(x * FY, FY), FY)
        there = pl.ds(pl.multiple_of((x + REACH) * FY, FY), FY)
        inv = look(ids_ref[here, :])
        inv_ref[there, :] = inv
        b_ref[there, :] = inv * fs_ref[here, :]
        return carry

    stores = []
    for c in range(CHUNKS):
        for copy in loads[c]:
            copy.wait()
        lax.fori_loop(c * step, (c + 1) * step, plane, 0, unroll=8)
        low = 0 if c == 0 else (c * step + REACH) * FY
        high = ((c + 1) * step + REACH + (REACH if c == CHUNKS - 1 else 0)) * FY
        part = pl.ds(low, high - low)
        for k, (src, dst) in enumerate(((b_ref, b_hbm), (inv_ref, inv_hbm))):
            copy = pltpu.make_async_copy(src.at[part], dst.at[part], osem.at[k, c])
            copy.start()
            stores.append(copy)
    zero = jnp.zeros((PAD, ROW), F32)
    for y in range(SWEEPS + 1):
        for src, dst in ((b_ref, bt_ref), (inv_ref, it_ref)):
            at = y * EXT
            dst[at : at + PAD] = zero
            dst[at + PAD + ROWS : at + EXT] = zero
            dst[at + PAD : at + PAD + ROWS] = src[pl.ds(REACH * FY + y, ROWS, stride=FY), :]
            for k in range(REACH):
                dst[at + PAD - REACH + k : at + PAD - REACH + k + 1] = src[
                    k * FY + y : k * FY + y + 1
                ]
                e = REACH + ROWS + k
                dst[at + PAD + ROWS + k : at + PAD + ROWS + k + 1] = src[
                    e * FY + y : e * FY + y + 1
                ]
    for copy in stores:
        copy.wait()


def wall_rows(recv_ref, poscol_ref):
    count = recv_ref.shape[0]
    wide = (EXT, count)
    slot = iota(wide, 1)
    kind = slot - SLOTS * lax.shift_right_logical(slot * 10923, 16)
    e = iota(wide, 0)
    halo = jnp.where(
        e < PAD,
        jnp.where(e >= PAD - REACH, e - (PAD - REACH) + 2, -1),
        jnp.where((e >= PAD + ROWS) & (e < PAD + ROWS + REACH), e - (PAD + ROWS) + 4, -1),
    )
    pos = poscol_ref[:, 0:1].astype(jnp.int32)
    hot = jnp.where((slot == pos) | (kind == halo), 1.0, 0.0)
    return dot(hot, recv_ref[...])


def along_row(s):
    lane = iota(s.shape, 1)
    last = s.shape[1] - 1
    low = jnp.where(lane == 0, 0.0, pltpu.roll(s, 1, axis=1))
    high = jnp.where(lane == last, 0.0, pltpu.roll(s, last, axis=1))
    return low + high


def thin_sweep(state, b, inv, depth):
    out = []
    for y in range(depth):
        s = state[y]
        total = pltpu.roll(s, EXT - 1, axis=0) + pltpu.roll(s, 1, axis=0)
        total = total + state[y + 1]
        if y > 0:
            total = total + state[y - 1]
        total = total + along_row(s)
        out.append(b[y] + inv[y] * total)
    return out


def send_traction(state, posrow_ref, tout_ref):
    traction = (state[0] - state[1])[PAD : PAD + ROWS]
    place = jnp.where(
        posrow_ref[0:1] == iota((tout_ref.shape[0], ROWS), 0).astype(F32), 1.0, 0.0
    )
    tout_ref[...] = dot(place, traction)


def thin_source(recv_ref, poscol_ref, bt_ref, it_ref, w_ref):
    w = wall_rows(recv_ref, poscol_ref)
    w_ref[...] = w
    inv = [it_ref[y * EXT : (y + 1) * EXT, :] for y in range(SWEEPS + 1)]
    b = [bt_ref[y * EXT : (y + 1) * EXT, :] for y in range(SWEEPS + 1)]
    b[0] = b[0] + w * inv[0]
    return b, inv


def thin_first_body(recv_ref, poscol_ref, posrow_ref, bt_ref, it_ref, tout_ref, w_ref):
    b, inv = thin_source(recv_ref, poscol_ref, bt_ref, it_ref, w_ref)
    state = thin_sweep(b, b, inv, 3)
    state = thin_sweep(state, b, inv, 2)
    send_traction(state, posrow_ref, tout_ref)


def thin_next_body(
    recv_ref, poscol_ref, posrow_ref, bt_ref, it_ref, st_ref, left_ref, right_ref, tout_ref,
    w_ref, ext_ref,
):
    zero = jnp.zeros((PAD, ROW), F32)
    for y in range(SWEEPS + 2):
        at = y * EXT
        ext_ref[at : at + PAD] = zero
        ext_ref[at + PAD + ROWS : at + EXT] = zero
        ext_ref[at + PAD : at + PAD + ROWS] = st_ref[y * ROWS : (y + 1) * ROWS]
        for k in range(SWEEPS):
            ext_ref[at + PAD - SWEEPS + k : at + PAD - SWEEPS + k + 1] = left_ref[
                k * FY + y : k * FY + y + 1
            ]
            ext_ref[at + PAD + ROWS + k : at + PAD + ROWS + k + 1] = right_ref[
                k * FY + y : k * FY + y + 1
            ]
    b, inv = thin_source(recv_ref, poscol_ref, bt_ref, it_ref, w_ref)
    state = [ext_ref[y * EXT : (y + 1) * EXT, :] for y in range(SWEEPS + 2)]
    state = thin_sweep(state, b, inv, 4)
    state = thin_sweep(state, b, inv, 3)
    state = thin_sweep(state, b, inv, 2)
    send_traction(state, posrow_ref, tout_ref)


def sweep(src_ref, shift, dst_ref, drop, b_ref, inv_ref, tri_ref, low, count, group):
    sub = iota((8, ROW), 0)

    def planes(g, carry):
        e = low + g * group
        base = pl.multiple_of(e * FY, FY)
        from_ = pl.multiple_of((e + shift) * FY, FY)
        to = pl.multiple_of((e - drop) * FY, FY)
        block = src_ref[pl.ds(from_, group * FY), :]
        coarse = block.astype(jnp.bfloat16)
        fine = (block - coarse.astype(F32)).astype(jnp.bfloat16)
        tri = tri_ref[...]
        along = jnp.dot(coarse, tri, preferred_element_type=F32)
        along = along + jnp.dot(fine, tri, preferred_element_type=F32)
        done = []
        for k in range(0, group * FY, 8):
            at = from_ + k
            total = src_ref[pl.ds(at - FY, 8), :] + src_ref[pl.ds(at + FY, 8), :]
            up, down = src_ref[pl.ds(at - 1, 8), :], src_ref[pl.ds(at + 1, 8), :]
            if k % FY == 0:
                up = jnp.where(sub == 0, 0.0, up)
            if k % FY == FY - 8:
                down = jnp.where(sub == 7, 0.0, down)
            total = total + (up + down)
            total = total + along[k : k + 8]
            done.append(b_ref[pl.ds(base + k, 8), :] + inv_ref[pl.ds(base + k, 8), :] * total)
        for k, value in enumerate(done):
            dst_ref[pl.ds(to + 8 * k, 8), :] = value
        return carry

    lax.fori_loop(0, count // group, planes, 0)


def fetch(pairs, sem):
    copies = [
        pltpu.make_async_copy(src, dst, sem.at[k]) for k, (src, dst) in enumerate(pairs)
    ]
    for copy in copies:
        copy.start()
    return copies


def halves(low, count):
    cut = count // 2
    return pl.ds(low * FY, cut * FY), pl.ds((low + cut) * FY, (count - cut) * FY)


def add_wall(b_ref, inv_ref, w_ref, first, planes):
    top = pl.ds(0, planes, stride=FY)
    b_ref[top, :] = b_ref[top, :] + inv_ref[top, :] * w_ref[first : first + planes, :]


def full_first_body(
    b_hbm, inv_hbm, w_ref, tri_ref, state_hbm, el_ref, er_ref, st_ref, tick_ref, b_ref, inv_ref,
    two_ref, out_ref, sem, osem,
):
    planes = ROWS + 2 * REACH
    pairs = []
    for part in halves(0, planes):
        pairs += [(b_hbm.at[part], b_ref.at[part]), (inv_hbm.at[part], inv_ref.at[part])]
    for copy in fetch(pairs, sem):
        copy.wait()
    add_wall(b_ref, inv_ref, w_ref, PAD - REACH, planes)
    sweep(b_ref, 0, two_ref, 0, b_ref, inv_ref, tri_ref, 1, ROWS + 2, 13)
    sweep(two_ref, 0, out_ref, REACH, b_ref, inv_ref, tri_ref, REACH, ROWS, 16)
    store = fetch([(out_ref.at[part], state_hbm.at[part]) for part in halves(0, ROWS)], osem)
    tick_ref[...] = jnp.zeros_like(tick_ref)
    el_ref[...] = out_ref[0 : SWEEPS * FY]
    er_ref[...] = out_ref[(ROWS - SWEEPS) * FY :]
    for y in range(SWEEPS + 2):
        st_ref[y * ROWS : (y + 1) * ROWS] = out_ref[pl.ds(y, ROWS, stride=FY), :]
    for copy in store:
        copy.wait()


def full_next_body(
    half, b_hbm, inv_hbm, w_ref, tri_ref, s_hbm, left_ref, right_ref, after_ref, out_hbm, tick_ref,
    b_ref, inv_ref, s_ref, two_ref, sem, osem,
):
    own = ROWS // 2
    first = half * own
    pairs = []
    planes = own + 2 * REACH
    for src, dst in zip(halves(first, planes), halves(0, planes)):
        pairs += [(b_hbm.at[src], b_ref.at[dst]), (inv_hbm.at[src], inv_ref.at[dst])]
    planes = own + SWEEPS
    low = max(first - SWEEPS, 0)
    at = SWEEPS if half == 0 else 0
    for src, dst in zip(halves(low, planes), halves(at, planes)):
        pairs.append((s_hbm.at[src], s_ref.at[dst]))
    copies = fetch(pairs, sem)
    if half == 0:
        s_ref[0 : SWEEPS * FY] = left_ref[...]
    else:
        s_ref[(own + SWEEPS) * FY : (own + 2 * SWEEPS) * FY] = right_ref[...]
    for copy in copies:
        copy.wait()
    add_wall(b_ref, inv_ref, w_ref, PAD - REACH + first, own + 2 * REACH)
    sweep(s_ref, 1, two_ref, 0, b_ref, inv_ref, tri_ref, 0, own + 4, 17)
    sweep(two_ref, 0, s_ref, 0, b_ref, inv_ref, tri_ref, 1, own + 2, 11)
    sweep(s_ref, 0, two_ref, REACH, b_ref, inv_ref, tri_ref, REACH, own, 16)
    pairs = []
    for src, dst in zip(halves(0, own), halves(first, own)):
        pairs.append((two_ref.at[src], out_hbm.at[dst]))
    store = fetch(pairs, osem)
    tick_ref[...] = jnp.zeros_like(tick_ref)
    for copy in store:
        copy.wait()


def full_second_body(
    b_hbm, inv_hbm, w_ref, tri_ref, s_hbm, left_ref, right_ref, after_ref, begun_hbm, *rest
):
    full_next_body(
        1, b_hbm, inv_hbm, w_ref, tri_ref, s_hbm, left_ref, right_ref, after_ref, *rest
    )


def exchange(buffer, devices):
    width = buffer.size // devices
    rows = buffer.reshape(devices, 1, width) if width != CAP * ROW else buffer.reshape(
        devices, CAP, ROW
    )
    got = lax.all_to_all(rows, AXES, split_axis=0, concat_axis=0, tiled=True)
    return got.reshape(buffer.shape)


def beside(to_right, to_left, devices):
    up = [(i, i + 1) for i in range(devices - 1)]
    down = [(i + 1, i) for i in range(devices - 1)]
    return lax.ppermute(to_right, AXES, up), lax.ppermute(to_left, AXES, down)


def buffers(*planes):
    return tuple(pltpu.VMEM((count * FY, ROW), F32) for count in planes)


def per_device(
    devices, fluid_source, coef_ids, coef_table, owner_device, owner_slot, solid_init, solid_load,
    compliance,
):
    fluid = fluid_source.reshape(ROWS * FY, ROW)
    ids = coef_ids.reshape(ROWS * FY, ROW)
    inverse = jnp.pad(1.0 / (6.0 + coef_table), (0, ROW - coef_table.shape[0]))
    inverse = jnp.broadcast_to(inverse[None, :], (8, ROW))
    tri = (jnp.eye(ROW, k=1) + jnp.eye(ROW, k=-1)).astype(jnp.bfloat16)
    edge = 2 * REACH
    dma = pltpu.SemaphoreType.DMA

    req, poscol, posrow = kernel_call(
        request_body, (shape(devices, ROW), shape(EXT, ROW), shape(8, ROWS)),
        owner_device.reshape(1, ROWS), owner_slot.reshape(1, ROWS), name="request",
    )
    wanted = exchange(req, devices)
    up, down = kernel_call(
        edges_body, (shape(edge * FY, ROW), shape(edge * FY, ROW)), fluid, ids, far=(0, 1),
        scratch=(pltpu.VMEM((2, REACH * FY, ROW), jnp.int32), dma((4,))), name="edges",
    )
    left, right = beside(up, down, devices)
    count = devices * SLOTS
    ans, sel, slotrow = kernel_call(
        functools.partial(pick_body, devices),
        (shape(count, ROW), shape(count, ROW), shape(8, CAP * devices)),
        wanted, solid_init, name="pick",
    )
    recv = exchange(ans, devices)
    wide = ROWS + 2 * REACH
    b, inv, bt, it = kernel_call(
        prepare_body,
        (shape(wide * FY, ROW), shape(wide * FY, ROW), shape(4 * EXT, ROW), shape(4 * EXT, ROW)),
        fluid, ids, inverse, left, right, slotrow, far=(0, 1), far_out=(0, 1),
        scratch=(
            *buffers(ROWS), pltpu.VMEM((ROWS * FY, ROW), jnp.int32), *buffers(wide, wide),
            dma((2, CHUNKS)), dma((2, CHUNKS)),
        ),
        flops=1e9, moved=1e7, name="prepare",
    )
    tout, w = kernel_call(
        thin_first_body, (shape(CAP * devices, ROW), shape(EXT, ROW)),
        recv, poscol, posrow, bt, it, name="thin0",
    )
    incoming = exchange(tout, devices)
    state, to_left, to_right, st, tick = kernel_call(
        full_first_body,
        (
            shape(ROWS * FY, ROW), shape(SWEEPS * FY, ROW), shape(SWEEPS * FY, ROW),
            shape((SWEEPS + 2) * ROWS, ROW), shape(8, ROW),
        ),
        b, inv, w, tri, far=(0, 1), far_out=(0,),
        scratch=(*buffers(wide, wide, wide, ROWS), dma((4,)), dma((2,))),
        flops=4e9, moved=1e7, name="full0",
    )
    ans, disp, part = kernel_call(
        solid_body, (shape(count, ROW), shape(ROWS, ROW), shape(8, ROW)),
        incoming, slotrow, solid_init, solid_load, compliance, sel, tick, name="solid0",
    )
    recv = exchange(ans, devices)
    left, right = beside(to_right, to_left, devices)
    tout, w = kernel_call(
        thin_next_body, (shape(CAP * devices, ROW), shape(EXT, ROW)),
        recv, poscol, posrow, bt, it, st, left, right,
        scratch=(pltpu.VMEM(((SWEEPS + 2) * EXT, ROW), F32),), name="thin1",
    )
    incoming = exchange(tout, devices)
    own = ROWS // 2
    scratch = (
        *buffers(own + 2 * REACH, own + 2 * REACH, own + 2 * SWEEPS, own + 2 * REACH),
        dma((6,)), dma((2,)),
    )
    begun, tick = kernel_call(
        functools.partial(full_next_body, 0), (shape(ROWS * FY, ROW), shape(8, ROW)),
        b, inv, w, tri, state, left, right, posrow, far=(0, 1, 4), far_out=(0,), scratch=scratch,
        flops=4e9, moved=1e7, name="full1",
    )
    disp, norm = kernel_call(
        functools.partial(last_body, devices), (shape(ROWS, ROW), shape(devices, ROW)),
        incoming, slotrow, disp, solid_load, compliance, part, tick, name="solid1",
    )
    norms = exchange(norm, devices)
    state, _ = kernel_call(
        full_second_body, (shape(ROWS * FY, ROW), shape(8, ROW)),
        b, inv, w, tri, state, left, right, disp, begun, far=(0, 1, 4, 8), far_out=(0,),
        alias={8: 0}, scratch=scratch, flops=4e9, moved=1e7, name="full2",
    )
    norms = jnp.sqrt(jnp.sum(norms[:, :COUPLE], axis=0) + 1e-06)
    return state.reshape(ROWS, FY, ROW), disp, norms


def solution(mesh):
    devices = mesh.shape["sect"] * mesh.shape["dom"]
    rows, planes = P(AXES, None), P(AXES, None, None)
    return jax.shard_map(
        functools.partial(per_device, devices),
        mesh=mesh,
        in_specs=(planes, planes, P(), rows, rows, rows, rows, P()),
        out_specs=(planes, rows, P()),
        check_vma=False,
    )
```
